32 devices in a mesh: member: 4 (over x, core), gx: 2 (over y), gy: 4 (over z).
Axes of the slice: x: 2, y: 2, z: 4, core: 2. Of those that a mesh axis runs over, the one named last changes fastest.
Arguments:
- tracers: float32 [8, 16, 128, 512], P('member', None, 'gx', 'gy'), may hold values from -6 to 6
- flux_x: float32 [16, 128, 512], P('member', 'gx', 'gy'), may hold values from -0.4 to 0.4
- flux_y: float32 [16, 128, 512], P('member', 'gx', 'gy'), may hold values from -0.4 to 0.4
- flux_z: float32 [16, 128, 512], P('member', 'gx', 'gy'), may hold values from -0.4 to 0.4
Outputs:
- transported: float32 [8, 16, 128, 512], P('member', None, 'gx', 'gy')
The draws below stay inside these ranges and needn't reach their ends.
All inputs are finite; a program needn't handle non-finite values.
Results may differ from the reference program's by a relative error of at most 0.0003.
Values sent between devices are 32-bit elements; how exact they have to be, the bound alone decides.
A program may use at most 128 MiB of HBM per device.

```python
import jax
import jax.numpy as jnp
from jax import lax

LEV = 16
TRACERS = 8
NX = 128
NY = 512


def block_scale(rng, extent, pieces, low, largest):
    factor_of = 1.0
    for position, blocks in pieces:
        draws = jax.random.uniform(jax.random.fold_in(jax.random.fold_in(rng, 6), position), (blocks,), jnp.float32, low / len(pieces), largest / len(pieces))
        factor_of = factor_of * jnp.repeat(jnp.exp(draws), extent[position] // blocks).reshape((-1,) + (1,) * (len(extent) - 1 - position))
    return factor_of


def noise(own_key, shape, scale, reach, shards=(), held_as=jnp.bfloat16):
    factor_of = block_scale(own_key, shape, shards, -0.22, 0.18) if shards else 1.0
    array = jax.random.normal(own_key, shape, jnp.float32) * scale * factor_of
    return jnp.minimum(jnp.maximum(array, -reach), reach).astype(held_as)


def setup_inputs(seed: int = 0) -> dict:
    splits = jax.random.split(jax.random.key(seed), 5)
    return {
        "tracers": noise(splits[0], (TRACERS, LEV, NX, NY), 1.0, 6.0, ((0, 4), (2, 2), (3, 4)), jnp.float32),
        "flux_x": jnp.clip(jax.random.uniform(splits[1], (LEV, NX, NY), jnp.float32, -0.4, 0.4) * block_scale(splits[1], (LEV, NX, NY), ((0, 4), (1, 2), (2, 4)), -0.4, 0.0), -0.4, 0.4),
        "flux_y": jnp.clip(jax.random.uniform(splits[2], (LEV, NX, NY), jnp.float32, -0.4, 0.4) * block_scale(splits[2], (LEV, NX, NY), ((0, 4), (1, 2), (2, 4)), -0.4, 0.0), -0.4, 0.4),
        "flux_z": jnp.clip(jax.random.uniform(splits[3], (LEV, NX, NY), jnp.float32, -0.4, 0.4) * block_scale(splits[3], (LEV, NX, NY), ((0, 4), (1, 2), (2, 4)), -0.4, 0.0), -0.4, 0.4),
    }


def advect(field, faces, axis):
    cells = faces.shape[axis] - 1

    def along(source, start, stop):
        return lax.slice_in_dim(source, start, stop, axis=axis)

    face_values = (7.0 * (along(field, 1, cells + 4) + along(field, 2, cells + 5)) - (along(field, 0, cells + 3) + along(field, 3, cells + 6))) / 12.0
    lower_a = along(face_values, 0, cells + 1)
    lower_b = along(face_values, 1, cells + 2)
    lower_mid = along(field, 2, cells + 3)
    upper_a = along(face_values, 1, cells + 2)
    upper_b = along(face_values, 2, cells + 3)
    upper_mid = along(field, 3, cells + 4)
    lower_d = lower_b - lower_a
    lower_h = 6.0 * lower_mid - 3.0 * (lower_a + lower_b)
    upper_d = upper_b - upper_a
    upper_h = 6.0 * upper_mid - 3.0 * (upper_a + upper_b)
    gauge = -faces
    from_lower = faces * (lower_b - 0.5 * faces * (lower_d - (1.0 - 2.0 * faces / 3.0) * lower_h))
    from_upper = faces * (upper_a + 0.5 * gauge * (upper_d + (1.0 - 2.0 * gauge / 3.0) * upper_h))
    face_flux = jnp.where(faces > 0, from_lower, from_upper)
    return along(field, 3, cells + 3) - (along(face_flux, 1, cells + 1) - along(face_flux, 0, cells))


def reference(tracers, flux_x, flux_y, flux_z):
    face_x = jnp.concatenate([flux_x[:, -1:, :], flux_x], axis=1)
    face_y = jnp.concatenate([flux_y[:, :, -1:], flux_y], axis=2)
    closed = jnp.zeros_like(flux_z[:1])
    face_z = jnp.concatenate([closed, flux_z[:-1], closed], axis=0)

    def advance(field):
        for step_index in range(2):
            field = advect(jnp.pad(field, ((0, 0), (3, 3), (0, 0)), mode="wrap"), face_x, 1)
            field = advect(jnp.pad(field, ((0, 0), (0, 0), (3, 3)), mode="wrap"), face_y, 2)
            field = advect(jnp.pad(field, ((3, 3), (0, 0), (0, 0)), mode="edge"), face_z, 0)
        return field

    return lax.map(advance, tracers)
```

```python
import functools

import jax
import jax.numpy as jnp
from jax import lax
from jax.experimental import pallas as pl
from jax.experimental.pallas import tpu as pltpu
from jax.sharding import PartitionSpec as P

MESH = pl.DeviceIdType.MESH
LANES = 128
GROUP = 8


def lane_roll(x, shift):
    return pltpu.roll(x, shift % LANES, 1)


def coefficients(c):
    s = jnp.abs(c)
    t = 1.0 - s
    ct = c * t * (1.0 / 12.0)
    return c > 0, ct * t, ct * s, c * s * (3.0 - 2.0 * s)


def flux(coefs, e, o, upwind):
    _, near, far, mean = coefs
    return near * e - far * o + mean * upwind


def lane_advect(q, coefs):
    positive = coefs[0]
    below = lane_roll(q, 1)
    p = below + q
    e = 8.0 * p - (lane_roll(p, 1) + lane_roll(p, -1))
    o = jnp.where(positive, lane_roll(e, 1), lane_roll(e, -1))
    f = flux(coefs, e, o, jnp.where(positive, below, q))
    return q - (lane_roll(f, -1) - f)


def kernel(
    sizes,
    tracers,
    flux_x,
    flux_y,
    flux_z,
    out,
    field0,
    field1,
    mid,
    fx,
    fy,
    fz,
    x_edge,
    y_edge,
    x_send,
    y_send,
    own_pack,
    to_right,
    to_left,
    from_left,
    from_right,
    face_left,
    face_right,
    face_flux,
    local_sem,
    wind_send,
    wind_recv,
    edge_send,
    edge_recv,
    halo_send,
    halo_recv,
    pack_send,
    pack_recv,
):
    members, n_x, n_y = sizes
    trac, levels, width_x, width_y = tracers.shape
    slab = levels // members
    groups = width_x // GROUP
    m = lax.axis_index("member")
    ix = lax.axis_index("gx")
    iy = lax.axis_index("gy")

    def member_of(j):
        if j == 0:
            return m
        if j == 1:
            return m + 1 - 2 * lax.rem(m, 2)
        if j == 2:
            return lax.rem(m + 2, 4)
        return 3 - m

    def device(j, dx, dy):
        return (member_of(j), lax.rem(ix + dx + n_x, n_x), lax.rem(iy + dy + n_y, n_y))

    x_steps = (1,) if n_x == 2 else (1, -1)
    y_steps = (1,) if n_y == 2 else (1, -1)
    partners = [(1, 0, 0), (2, 0, 0)]
    partners += [(j, d, 0) for j in range(4) for d in x_steps]
    partners += [(j, 0, d) for j in range(4) for d in y_steps]
    barrier = pltpu.get_barrier_semaphore()
    for partner in partners:
        pl.semaphore_signal(barrier, inc=1, device_id=device(*partner), device_id_type=MESH)

    def levels_of(j):
        return pl.ds(member_of(j) * slab, slab)

    inner = pl.ds(GROUP, width_x)
    winds = ((flux_x, fx), (flux_y, fy), (flux_z, fz))

    def wind_dst(k, j):
        if k == 0:
            return fx.at[levels_of(j), inner, :]
        return winds[k][1].at[levels_of(j), :, :]

    locals_ = [
        pltpu.make_async_copy(winds[k][0], wind_dst(k, 0), local_sem.at[k]) for k in range(3)
    ]
    load = pltpu.make_async_copy(tracers, field0.at[:, :, inner, :], local_sem.at[3])
    locals_[0].start()
    locals_[1].start()
    load.start()
    locals_[2].start()
    pl.semaphore_wait(barrier, len(partners))

    def remote(src, dst, send, recv, dev):
        return pltpu.make_async_remote_copy(
            src_ref=src, dst_ref=dst, send_sem=send, recv_sem=recv, device_id=dev, device_id_type=MESH
        )

    def halo_copies(step, j):
        target = (field0, field1)[step]
        ls = levels_of(j)
        if step == 0:
            low_src = tracers.at[:, ls, pl.ds(0, GROUP), :]
            high_src = tracers.at[:, ls, pl.ds(width_x - GROUP, GROUP), :]
        else:
            low_src = field1.at[:, ls, pl.ds(GROUP, GROUP), :]
            high_src = field1.at[:, ls, pl.ds(width_x, GROUP), :]
        return (
            remote(
                high_src,
                target.at[:, ls, pl.ds(0, GROUP), :],
                halo_send.at[step, j, 0],
                halo_recv.at[step, j, 0],
                device(0, 1, 0),
            ),
            remote(
                low_src,
                target.at[:, ls, pl.ds(width_x + GROUP, GROUP), :],
                halo_send.at[step, j, 1],
                halo_recv.at[step, j, 1],
                device(0, -1, 0),
            ),
        )

    halos = [[halo_copies(step, j) for j in range(4)] for step in range(2)]
    direct = [[remote(winds[k][0], wind_dst(k, 0), wind_send.at[j - 1, k], wind_recv.at[j - 1, k], device(j, 0, 0))
               for k in range(3)] for j in (1, 2)]
    relay = [
        remote(wind_dst(k, 2), wind_dst(k, 2), wind_send.at[2, k], wind_recv.at[2, k], device(1, 0, 0))
        for k in range(3)
    ]
    for j in range(4):
        for c in halos[0][j]:
            c.start()
    for k in range(3):
        direct[1][k].start()
        direct[0][k].start()

    lane = lax.broadcasted_iota(jnp.int32, (GROUP, LANES), 1)
    window = lax.rem(lane, 16)
    low_half = window < 8
    at_edge = (lane < 3) | (lane >= LANES - 3)

    def in_window(g):
        return (lane >= 16 * g) & (lane < 16 * g + 16)

    def packed(pieces):
        total = lane_roll(pieces[0], 8)
        for g in range(1, groups):
            total = jnp.where(in_window(g), lane_roll(pieces[g], 8 + 16 * g), total)
        return total

    locals_[0].wait()
    locals_[1].wait()
    column = jnp.zeros((GROUP, LANES), jnp.float32)
    for k in range(slab):
        x_send[pl.ds(k, 1), :] = fx[m * slab + k, pl.ds(width_x + GROUP - 1, 1), :]
        piece = packed([fy[m * slab + k, pl.ds(GROUP * g, GROUP), :] for g in range(groups)])
        column = jnp.where(window == 4 + k, lane_roll(piece, k - 3), column)
    y_send[...] = column
    edges = []
    for j in range(4):
        edges.append(remote(x_send, x_edge.at[m], edge_send.at[0, j], edge_recv.at[0, j], device(j, 1, 0)))
        edges.append(remote(y_send, y_edge.at[m], edge_send.at[1, j], edge_recv.at[1, j], device(j, 0, 1)))
    for c in edges:
        c.start()

    def wait_edge(axis, j):
        edges[2 * j + axis].wait_recv()

    def wait_wind(k, j):
        if j == 0:
            if k == 2:
                locals_[2].wait()
        elif j == 3:
            relay[k].wait_recv()
        else:
            direct[j - 1][k].wait_recv()

    def pack_copies(step, j):
        ls = levels_of(j)
        return (
            remote(
                to_right.at[step, ls],
                from_left.at[step, ls],
                pack_send.at[step, j, 0],
                pack_recv.at[step, j, 0],
                device(0, 0, 1),
            ),
            remote(
                to_left.at[step, ls],
                from_right.at[step, ls],
                pack_send.at[step, j, 1],
                pack_recv.at[step, j, 1],
                device(0, 0, -1),
            ),
        )

    packs = [[pack_copies(step, j) for j in range(4)] for step in range(2)]

    def sweep_x(step, j):
        field = (field0, field1)[step]
        first = member_of(j) * slab

        def one_level(k, carry):
            level = first + k
            for start in [GROUP * g for g in range(groups)] + [width_x - GROUP + 1]:
                coefs = coefficients(fx[level, pl.ds(GROUP - 1 + start, GROUP), :])
                positive = coefs[0]
                for t in range(trac):
                    q = [field[t, level, pl.ds(GROUP + start + s, GROUP), :] for s in range(-3, 3)]
                    p = [q[i] + q[i + 1] for i in range(5)]
                    e = 8.0 * p[2] - (p[1] + p[3])
                    o = 8.0 * jnp.where(positive, p[1], p[3]) - (jnp.where(positive, p[0], p[4]) + p[2])
                    face_flux[t, pl.ds(start, GROUP), :] = flux(coefs, e, o, jnp.where(positive, q[2], q[3]))
            packs_here = []
            for t in range(trac):
                pieces = []
                for g in range(groups):
                    new = field[t, level, pl.ds(GROUP + GROUP * g, GROUP), :] - (
                        face_flux[t, pl.ds(GROUP * g + 1, GROUP), :] - face_flux[t, pl.ds(GROUP * g, GROUP), :]
                    )
                    mid[t, level, pl.ds(GROUP * g, GROUP), :] = new
                    pieces.append(new)
                both = packed(pieces)
                own_pack[t, level] = both
                packs_here.append(both)
            to_right[step, level] = jnp.where(low_half, packs_here[0], lane_roll(packs_here[1], 8))
            to_left[step, level] = jnp.where(low_half, lane_roll(packs_here[1], -8), packs_here[0])
            return carry

        lax.fori_loop(0, slab, one_level, 0)

    def sweep_y(step, j):
        first = member_of(j) * slab

        def one_level(k, carry):
            level = first + k
            if step == 0:
                rows = [fy[level, pl.ds(GROUP * g, GROUP), :] for g in range(groups)]
                right = lane_roll(packed(rows), 1)
                outer = pltpu.roll(y_edge[member_of(j)], 4 - k, 1)
                left = jnp.where(window == 8, outer, right)
                face_left[level] = left
                face_right[level] = right
            else:
                left = face_left[level]
                right = face_right[level]
            left = coefficients(left)
            right = coefficients(right)
            left_in = from_left[step, level]
            right_in = from_right[step, level]
            fixed = []
            for t in range(trac):
                own = own_pack[t, level]
                lower = left_in if t == 0 else lane_roll(left_in, -8)
                upper = right_in if t == 0 else lane_roll(right_in, 8)
                at_left = lane_advect(jnp.where(low_half, lower, own), left)
                at_right = lane_advect(jnp.where(low_half, own, upper), right)
                fixed.append(jnp.where(low_half, at_right, at_left))
            for g in range(groups):
                coefs = coefficients(lane_roll(fy[level, pl.ds(GROUP * g, GROUP), :], 1))
                for t in range(trac):
                    new = lane_advect(mid[t, level, pl.ds(GROUP * g, GROUP), :], coefs)
                    mid[t, level, pl.ds(GROUP * g, GROUP), :] = jnp.where(
                        at_edge, lane_roll(fixed[t], -(8 + 16 * g)), new
                    )
            return carry

        lax.fori_loop(0, slab, one_level, 0)

    def sweep_z(step, row):
        q = {}
        p = {}
        e = {}
        before = {}

        def cell(t, l):
            l = min(max(l, 0), levels - 1)
            if (t, l) not in q:
                q[t, l] = mid[t, l, pl.ds(row, GROUP), :]
            return q[t, l]

        def pair(t, l):
            if (t, l) not in p:
                p[t, l] = cell(t, l - 1) + cell(t, l)
            return p[t, l]

        def edge(t, l):
            if (t, l) not in e:
                e[t, l] = 8.0 * pair(t, l) - (pair(t, l - 1) + pair(t, l + 1))
            return e[t, l]

        for l in range(levels):
            if l + 1 < levels:
                coefs = coefficients(fz[l, pl.ds(row, GROUP), :])
            for t in range(trac):
                new = cell(t, l)
                if l > 0:
                    new = new + before[t]
                if l + 1 < levels:
                    positive = coefs[0]
                    o = jnp.where(positive, edge(t, l), edge(t, l + 2))
                    f = flux(coefs, edge(t, l + 1), o, jnp.where(positive, cell(t, l), cell(t, l + 1)))
                    new = new - f
                    before[t] = f
                if step == 0:
                    field1[t, l, pl.ds(GROUP + row, GROUP), :] = new
                else:
                    out[t, l, pl.ds(row, GROUP), :] = new

    def sweep_z_groups(step, start, stop):
        def one_group(g, carry):
            sweep_z(step, pl.multiple_of(g * GROUP, GROUP))
            return carry

        lax.fori_loop(start, stop, one_group, 0)

    def exchange(k):
        direct[1][k].wait_recv()
        relay[k].start()

    load.wait()
    for j in range(4):
        for c in halos[0][j]:
            c.wait_recv()
        if j == 1:
            exchange(0)
        if j != 2:
            wait_wind(0, j)
        wait_edge(0, j)
        source = member_of(j)
        for k in range(slab):
            fx[source * slab + k, pl.ds(GROUP - 1, 1), :] = x_edge[source, pl.ds(k, 1), :]
        sweep_x(0, j)
        for c in packs[0][j]:
            c.start()
    for j in range(4):
        wait_edge(1, j)
        if j == 2:
            exchange(1)
        if j != 2:
            wait_wind(1, j)
        for c in packs[0][j]:
            c.wait_recv()
        sweep_y(0, j)
    exchange(2)
    for j in (0, 1, 3):
        wait_wind(2, j)
    sweep_z(0, 0)
    sweep_z(0, width_x - GROUP)
    for j in range(4):
        for c in halos[1][j]:
            c.start()
    sweep_z_groups(0, 1, groups - 1)

    for j in range(4):
        for c in halos[1][j]:
            c.wait_recv()
        sweep_x(1, j)
        for c in packs[1][j]:
            c.start()
    for j in range(4):
        for c in packs[1][j]:
            c.wait_recv()
        sweep_y(1, j)
    sweep_z_groups(1, 0, groups)

    for step in range(2):
        for j in range(4):
            for c in halos[step][j] + packs[step][j]:
                c.wait_send()
    for c in direct[0] + direct[1] + relay + edges:
        c.wait_send()


def body(sizes, tracers, flux_x, flux_y, flux_z):
    trac, levels, width_x, width_y = tracers.shape[0], tracers.shape[1], tracers.shape[2], tracers.shape[3]
    members = sizes[0]
    packed = pltpu.VMEM((2, levels, GROUP, LANES), jnp.float32)
    return pl.pallas_call(
        functools.partial(kernel, sizes),
        out_shape=jax.ShapeDtypeStruct(tracers.shape, jnp.float32),
        in_specs=[pl.BlockSpec(memory_space=pl.ANY)] * 4,
        out_specs=pl.BlockSpec(memory_space=pltpu.VMEM),
        scratch_shapes=[
            pltpu.VMEM((trac, levels, width_x + 2 * GROUP, width_y), jnp.float32),
            pltpu.VMEM((trac, levels, width_x + 2 * GROUP, width_y), jnp.float32),
            pltpu.VMEM((trac, levels, width_x, width_y), jnp.float32),
            pltpu.VMEM((levels, width_x + GROUP, width_y), jnp.float32),
            pltpu.VMEM((levels, width_x, width_y), jnp.float32),
            pltpu.VMEM((levels, width_x, width_y), jnp.float32),
            pltpu.VMEM((members, GROUP, LANES), jnp.float32),
            pltpu.VMEM((members, GROUP, LANES), jnp.float32),
            pltpu.VMEM((GROUP, LANES), jnp.float32),
            pltpu.VMEM((GROUP, LANES), jnp.float32),
            pltpu.VMEM((trac, levels, GROUP, LANES), jnp.float32),
            packed,
            packed,
            packed,
            packed,
            pltpu.VMEM((levels, GROUP, LANES), jnp.float32),
            pltpu.VMEM((levels, GROUP, LANES), jnp.float32),
            pltpu.VMEM((trac, width_x + GROUP, width_y), jnp.float32),
            pltpu.SemaphoreType.DMA((4,)),
            pltpu.SemaphoreType.DMA((3, 3)),
            pltpu.SemaphoreType.DMA((3, 3)),
            pltpu.SemaphoreType.DMA((2, 4)),
            pltpu.SemaphoreType.DMA((2, 4)),
            pltpu.SemaphoreType.DMA((2, 4, 2)),
            pltpu.SemaphoreType.DMA((2, 4, 2)),
            pltpu.SemaphoreType.DMA((2, 4, 2)),
            pltpu.SemaphoreType.DMA((2, 4, 2)),
        ],
        compiler_params=pltpu.CompilerParams(
            collective_id=0, has_side_effects=True, vmem_limit_bytes=48 * 1024 * 1024
        ),
    )(tracers, flux_x, flux_y, flux_z)


def solution(mesh):
    sizes = (mesh.shape["member"], mesh.shape["gx"], mesh.shape["gy"])
    return jax.shard_map(
        functools.partial(body, sizes),
        mesh=mesh,
        in_specs=(
            P("member", None, "gx", "gy"),
            P("member", "gx", "gy"),
            P("member", "gx", "gy"),
            P("member", "gx", "gy"),
        ),
        out_specs=P("member", None, "gx", "gy"),
        check_vma=False,
    )
```

```python
import functools

import jax
import jax.numpy as jnp
from jax import lax
from jax.experimental import pallas as pl
from jax.experimental.pallas import tpu as pltpu
from jax.sharding import PartitionSpec as P

MESH = pl.DeviceIdType.MESH
LANES = 128
GROUP = 8
RIM = 3


def lane_roll(x, shift):
    return pltpu.roll(x, shift % LANES, 1)


def coefficients(c):
    s = jnp.abs(c)
    t = 1.0 - s
    ct = c * t * (1.0 / 12.0)
    return c > 0, ct * t, ct * s, c * s * (3.0 - 2.0 * s)


def flux(coefs, e, o, upwind):
    _, near, far, mean = coefs
    return near * e - far * o + mean * upwind


def lane_advect(q, products, coefs):
    e, e_below, e_above, below = products
    positive = coefs[0]
    f = flux(coefs, e, jnp.where(positive, e_below, e_above), jnp.where(positive, below, q))
    return q - (lane_roll(f, -1) - f)


def stencil_matrix(shape):
    cell = lax.rem(lax.broadcasted_iota(jnp.int32, shape, 0), LANES)
    column = lax.broadcasted_iota(jnp.int32, shape, 1)
    face = lax.rem(column, LANES)
    part = column // LANES
    base = jnp.where(part == 1, -1, jnp.where(part == 2, 1, 0))
    offset = lax.rem(cell - face - base + 2 * LANES, LANES)
    edge = jnp.where((offset == 0) | (offset == LANES - 1), 7.0, 0.0) - jnp.where(
        (offset == 1) | (offset == LANES - 2), 1.0, 0.0
    )
    shifted = jnp.where(offset == LANES - 1, 1.0, 0.0)
    return jnp.where(part == 3, shifted, edge)


def kernel(
    sizes,
    tracers,
    flux_x,
    flux_y,
    flux_z,
    out,
    field0,
    field1,
    mid,
    fx,
    fy,
    fz,
    x_edge,
    y_edge,
    x_send,
    y_send,
    own_pack,
    to_right,
    to_left,
    from_left,
    from_right,
    face_left,
    face_right,
    face_flux,
    stencil,
    halves,
    products,
    local_sem,
    wind_send,
    wind_recv,
    edge_send,
    edge_recv,
    halo_send,
    halo_recv,
    pack_send,
    pack_recv,
):
    members, n_x, n_y = sizes
    trac, levels, width_x, width_y = tracers.shape
    slab = levels // members
    groups = width_x // GROUP
    m = lax.axis_index("member")
    ix = lax.axis_index("gx")
    iy = lax.axis_index("gy")

    def member_of(j):
        if j == 0:
            return m
        if j == 1:
            return m + 1 - 2 * lax.rem(m, 2)
        if j == 2:
            return lax.rem(m + 2, 4)
        return 3 - m

    def device(j, dx, dy):
        return (member_of(j), lax.rem(ix + dx + n_x, n_x), lax.rem(iy + dy + n_y, n_y))

    x_steps = (1,) if n_x == 2 else (1, -1)
    y_steps = (1,) if n_y == 2 else (1, -1)
    partners = [(1, 0, 0), (2, 0, 0)]
    partners += [(j, d, 0) for j in range(4) for d in x_steps]
    partners += [(j, 0, d) for j in range(4) for d in y_steps]
    barrier = pltpu.get_barrier_semaphore()
    for partner in partners:
        pl.semaphore_signal(barrier, inc=1, device_id=device(*partner), device_id_type=MESH)

    def levels_of(j):
        return pl.ds(member_of(j) * slab, slab)

    inner = pl.ds(GROUP, width_x)
    winds = ((flux_x, fx), (flux_y, fy), (flux_z, fz))

    def wind_dst(k, j):
        if k == 0:
            return fx.at[levels_of(j), inner, :]
        return winds[k][1].at[levels_of(j), :, :]

    locals_ = [
        pltpu.make_async_copy(winds[k][0], wind_dst(k, 0), local_sem.at[k]) for k in range(3)
    ]
    load = pltpu.make_async_copy(tracers, field0.at[:, :, inner, :], local_sem.at[3])
    locals_[0].start()
    locals_[1].start()
    load.start()
    locals_[2].start()
    stencil[...] = stencil_matrix(stencil.shape).astype(jnp.bfloat16)
    pl.semaphore_wait(barrier, len(partners))

    def remote(src, dst, send, recv, dev):
        return pltpu.make_async_remote_copy(
            src_ref=src, dst_ref=dst, send_sem=send, recv_sem=recv, device_id=dev, device_id_type=MESH
        )

    def halo_copies(step, j):
        target = (field0, field1)[step]
        ls = levels_of(j)
        if step == 0:
            low_src = tracers.at[:, ls, pl.ds(0, RIM), :]
            high_src = tracers.at[:, ls, pl.ds(width_x - RIM, RIM), :]
        else:
            low_src = field1.at[:, ls, pl.ds(GROUP, RIM), :]
            high_src = field1.at[:, ls, pl.ds(GROUP + width_x - RIM, RIM), :]
        return (
            remote(
                high_src,
                target.at[:, ls, pl.ds(GROUP - RIM, RIM), :],
                halo_send.at[step, j, 0],
                halo_recv.at[step, j, 0],
                device(0, 1, 0),
            ),
            remote(
                low_src,
                target.at[:, ls, pl.ds(width_x + GROUP, RIM), :],
                halo_send.at[step, j, 1],
                halo_recv.at[step, j, 1],
                device(0, -1, 0),
            ),
        )

    halos = [[halo_copies(step, j) for j in range(4)] for step in range(2)]
    direct = [[remote(winds[k][0], wind_dst(k, 0), wind_send.at[j - 1, k], wind_recv.at[j - 1, k], device(j, 0, 0))
               for k in range(3)] for j in (1, 2)]
    relay = [
        remote(wind_dst(k, 2), wind_dst(k, 2), wind_send.at[2, k], wind_recv.at[2, k], device(1, 0, 0))
        for k in range(3)
    ]
    for j in range(4):
        for c in halos[0][j]:
            c.start()
    for k in range(3):
        direct[1][k].start()
        direct[0][k].start()

    lane = lax.broadcasted_iota(jnp.int32, (GROUP, LANES), 1)
    window = lax.rem(lane, 16)
    low_half = window < 8
    at_edge = (lane < 3) | (lane >= LANES - 3)

    def in_window(g):
        return (lane >= 16 * g) & (lane < 16 * g + 16)

    def packed(pieces):
        total = lane_roll(pieces[0], 8)
        for g in range(1, groups):
            total = jnp.where(in_window(g), lane_roll(pieces[g], 8 + 16 * g), total)
        return total

    locals_[0].wait()
    locals_[1].wait()
    column = jnp.zeros((GROUP, LANES), jnp.float32)
    for k in range(slab):
        x_send[pl.ds(k, 1), :] = fx[m * slab + k, pl.ds(width_x + GROUP - 1, 1), :]
        piece = packed([fy[m * slab + k, pl.ds(GROUP * g, GROUP), :] for g in range(groups)])
        column = jnp.where(window == 4 + k, lane_roll(piece, k - 3), column)
    y_send[...] = column
    edges = []
    for j in range(4):
        edges.append(remote(x_send, x_edge.at[m], edge_send.at[0, j], edge_recv.at[0, j], device(j, 1, 0)))
        edges.append(remote(y_send, y_edge.at[m], edge_send.at[1, j], edge_recv.at[1, j], device(j, 0, 1)))
    for c in edges:
        c.start()

    def wait_edge(axis, j):
        edges[2 * j + axis].wait_recv()

    def wait_wind(k, j):
        if j == 0:
            if k == 2:
                locals_[2].wait()
        elif j == 3:
            relay[k].wait_recv()
        else:
            direct[j - 1][k].wait_recv()

    def pack_copies(step, j):
        ls = levels_of(j)
        return (
            remote(
                to_right.at[step, ls],
                from_left.at[step, ls],
                pack_send.at[step, j, 0],
                pack_recv.at[step, j, 0],
                device(0, 0, 1),
            ),
            remote(
                to_left.at[step, ls],
                from_right.at[step, ls],
                pack_send.at[step, j, 1],
                pack_recv.at[step, j, 1],
                device(0, 0, -1),
            ),
        )

    packs = [[pack_copies(step, j) for j in range(4)] for step in range(2)]

    def sweep_x(step, j):
        field = (field0, field1)[step]
        first = member_of(j) * slab

        def one_level(k, carry):
            level = first + k
            for start in [GROUP * g for g in range(groups)] + [width_x - GROUP + 1]:
                coefs = coefficients(fx[level, pl.ds(GROUP - 1 + start, GROUP), :])
                positive = coefs[0]
                for t in range(trac):
                    q = [field[t, level, pl.ds(GROUP + start + s, GROUP), :] for s in range(-3, 3)]
                    p = [q[i] + q[i + 1] for i in range(5)]
                    e = 8.0 * p[2] - (p[1] + p[3])
                    o = 8.0 * jnp.where(positive, p[1], p[3]) - (jnp.where(positive, p[0], p[4]) + p[2])
                    face_flux[t, pl.ds(start, GROUP), :] = flux(coefs, e, o, jnp.where(positive, q[2], q[3]))
            packs_here = []
            for t in range(trac):
                pieces = []
                for g in range(groups):
                    new = field[t, level, pl.ds(GROUP + GROUP * g, GROUP), :] - (
                        face_flux[t, pl.ds(GROUP * g + 1, GROUP), :] - face_flux[t, pl.ds(GROUP * g, GROUP), :]
                    )
                    mid[t, level, pl.ds(GROUP * g, GROUP), :] = new
                    pieces.append(new)
                both = packed(pieces)
                own_pack[t, level] = both
                packs_here.append(both)
            to_right[step, level] = jnp.where(low_half, packs_here[0], lane_roll(packs_here[1], 8))
            to_left[step, level] = jnp.where(low_half, lane_roll(packs_here[1], -8), packs_here[0])
            return carry

        lax.fori_loop(0, slab, one_level, 0)

    per_level = trac * (width_x + 2 * GROUP)

    def sweep_y(step, j):
        first = member_of(j) * slab

        def put(row, x):
            high = x.astype(jnp.bfloat16)
            low = (x - high.astype(jnp.float32)).astype(jnp.bfloat16)
            rows = pl.ds(pl.multiple_of(row, 16), 16)
            halves[rows, pl.ds(0, LANES)] = high
            halves[rows, pl.ds(LANES, LANES)] = low

        def windows(level):
            left_in = from_left[step, level]
            right_in = from_right[step, level]
            result = []
            for t in range(trac):
                own = own_pack[t, level]
                lower = left_in if t == 0 else lane_roll(left_in, -8)
                upper = right_in if t == 0 else lane_roll(right_in, 8)
                result.append((jnp.where(low_half, lower, own), jnp.where(low_half, own, upper)))
            return result

        def split(k, carry):
            level = first + k
            start = k * per_level
            for t in range(trac):
                for r in range(width_x // 16):
                    put(start + t * width_x + 16 * r, mid[t, level, pl.ds(16 * r, 16), :])
            for t, pair in enumerate(windows(level)):
                put(start + trac * width_x + 16 * t, jnp.concatenate(pair, axis=0))
            return carry

        lax.fori_loop(0, slab, split, 0)
        products[...] = jnp.dot(halves[...], stencil[...], preferred_element_type=jnp.float32)

        def one_level(k, carry):
            level = first + k
            start = k * per_level
            if step == 0:
                rows = [fy[level, pl.ds(GROUP * g, GROUP), :] for g in range(groups)]
                right = lane_roll(packed(rows), 1)
                outer = pltpu.roll(y_edge[member_of(j)], 4 - k, 1)
                left = jnp.where(window == 8, outer, right)
                face_left[level] = left
                face_right[level] = right
            else:
                left = face_left[level]
                right = face_right[level]
            left = coefficients(left)
            right = coefficients(right)

            def parts(row):
                rows = pl.ds(pl.multiple_of(start + row, GROUP), GROUP)
                return [products[rows, pl.ds(LANES * i, LANES)] for i in range(4)]

            fixed = []
            for t, (at_left, at_right) in enumerate(windows(level)):
                row = trac * width_x + 16 * t
                at_left = lane_advect(at_left, parts(row), left)
                at_right = lane_advect(at_right, parts(row + GROUP), right)
                fixed.append(jnp.where(low_half, at_right, at_left))
            for g in range(groups):
                coefs = coefficients(lane_roll(fy[level, pl.ds(GROUP * g, GROUP), :], 1))
                for t in range(trac):
                    rows = pl.ds(GROUP * g, GROUP)
                    new = lane_advect(mid[t, level, rows, :], parts(t * width_x + GROUP * g), coefs)
                    mid[t, level, rows, :] = jnp.where(at_edge, lane_roll(fixed[t], -(8 + 16 * g)), new)
            return carry

        lax.fori_loop(0, slab, one_level, 0)

    def sweep_z(step, row):
        q = {}
        p = {}
        e = {}
        before = {}

        def cell(t, l):
            l = min(max(l, 0), levels - 1)
            if (t, l) not in q:
                q[t, l] = mid[t, l, pl.ds(row, GROUP), :]
            return q[t, l]

        def pair(t, l):
            if (t, l) not in p:
                p[t, l] = cell(t, l - 1) + cell(t, l)
            return p[t, l]

        def edge(t, l):
            if (t, l) not in e:
                e[t, l] = 8.0 * pair(t, l) - (pair(t, l - 1) + pair(t, l + 1))
            return e[t, l]

        for l in range(levels):
            if l + 1 < levels:
                coefs = coefficients(fz[l, pl.ds(row, GROUP), :])
            for t in range(trac):
                new = cell(t, l)
                if l > 0:
                    new = new + before[t]
                if l + 1 < levels:
                    positive = coefs[0]
                    o = jnp.where(positive, edge(t, l), edge(t, l + 2))
                    f = flux(coefs, edge(t, l + 1), o, jnp.where(positive, cell(t, l), cell(t, l + 1)))
                    new = new - f
                    before[t] = f
                if step == 0:
                    field1[t, l, pl.ds(GROUP + row, GROUP), :] = new
                else:
                    out[t, l, pl.ds(row, GROUP), :] = new

    def sweep_z_groups(step, start, stop):
        def one_group(g, carry):
            sweep_z(step, pl.multiple_of(g * GROUP, GROUP))
            return carry

        lax.fori_loop(start, stop, one_group, 0)

    def exchange(k):
        direct[1][k].wait_recv()
        relay[k].start()

    load.wait()
    for j in range(4):
        for c in halos[0][j]:
            c.wait_recv()
        if j == 1:
            exchange(0)
        if j != 2:
            wait_wind(0, j)
        wait_edge(0, j)
        source = member_of(j)
        for k in range(slab):
            fx[source * slab + k, pl.ds(GROUP - 1, 1), :] = x_edge[source, pl.ds(k, 1), :]
        sweep_x(0, j)
        for c in packs[0][j]:
            c.start()
    for j in range(4):
        wait_edge(1, j)
        if j == 2:
            exchange(1)
        if j != 2:
            wait_wind(1, j)
        for c in packs[0][j]:
            c.wait_recv()
        sweep_y(0, j)
    exchange(2)
    for j in (0, 1, 3):
        wait_wind(2, j)
    sweep_z(0, 0)
    sweep_z(0, width_x - GROUP)
    for j in range(4):
        for c in halos[1][j]:
            c.start()
    sweep_z_groups(0, 1, groups - 1)

    for j in range(4):
        for c in halos[1][j]:
            c.wait_recv()
        sweep_x(1, j)
        for c in packs[1][j]:
            c.start()
    for j in range(4):
        for c in packs[1][j]:
            c.wait_recv()
        sweep_y(1, j)
    sweep_z_groups(1, 0, groups)

    for step in range(2):
        for j in range(4):
            for c in halos[step][j] + packs[step][j]:
                c.wait_send()
    for c in direct[0] + direct[1] + relay + edges:
        c.wait_send()


def body(sizes, tracers, flux_x, flux_y, flux_z):
    trac, levels, width_x, width_y = tracers.shape[0], tracers.shape[1], tracers.shape[2], tracers.shape[3]
    members = sizes[0]
    matrix_rows = levels // members * trac * (width_x + 2 * GROUP)
    packed = pltpu.VMEM((2, levels, GROUP, LANES), jnp.float32)
    return pl.pallas_call(
        functools.partial(kernel, sizes),
        out_shape=jax.ShapeDtypeStruct(tracers.shape, jnp.float32),
        in_specs=[pl.BlockSpec(memory_space=pltpu.HBM)] * 4,
        out_specs=pl.BlockSpec(memory_space=pltpu.VMEM),
        scratch_shapes=[
            pltpu.VMEM((trac, levels, width_x + 2 * GROUP, width_y), jnp.float32),
            pltpu.VMEM((trac, levels, width_x + 2 * GROUP, width_y), jnp.float32),
            pltpu.VMEM((trac, levels, width_x, width_y), jnp.float32),
            pltpu.VMEM((levels, width_x + GROUP, width_y), jnp.float32),
            pltpu.VMEM((levels, width_x, width_y), jnp.float32),
            pltpu.VMEM((levels, width_x, width_y), jnp.float32),
            pltpu.VMEM((members, GROUP, LANES), jnp.float32),
            pltpu.VMEM((members, GROUP, LANES), jnp.float32),
            pltpu.VMEM((GROUP, LANES), jnp.float32),
            pltpu.VMEM((GROUP, LANES), jnp.float32),
            pltpu.VMEM((trac, levels, GROUP, LANES), jnp.float32),
            packed,
            packed,
            packed,
            packed,
            pltpu.VMEM((levels, GROUP, LANES), jnp.float32),
            pltpu.VMEM((levels, GROUP, LANES), jnp.float32),
            pltpu.VMEM((trac, width_x + GROUP, width_y), jnp.float32),
            pltpu.VMEM((2 * LANES, 4 * LANES), jnp.bfloat16),
            pltpu.VMEM((matrix_rows, 2 * LANES), jnp.bfloat16),
            pltpu.VMEM((matrix_rows, 4 * LANES), jnp.float32),
            pltpu.SemaphoreType.DMA((4,)),
            pltpu.SemaphoreType.DMA((3, 3)),
            pltpu.SemaphoreType.DMA((3, 3)),
            pltpu.SemaphoreType.DMA((2, 4)),
            pltpu.SemaphoreType.DMA((2, 4)),
            pltpu.SemaphoreType.DMA((2, 4, 2)),
            pltpu.SemaphoreType.DMA((2, 4, 2)),
            pltpu.SemaphoreType.DMA((2, 4, 2)),
            pltpu.SemaphoreType.DMA((2, 4, 2)),
        ],
        compiler_params=pltpu.CompilerParams(
            collective_id=0, has_side_effects=True
        ),
    )(tracers, flux_x, flux_y, flux_z)


def solution(mesh):
    sizes = (mesh.shape["member"], mesh.shape["gx"], mesh.shape["gy"])
    return jax.shard_map(
        functools.partial(body, sizes),
        mesh=mesh,
        in_specs=(
            P("member", None, "gx", "gy"),
            P("member", "gx", "gy"),
            P("member", "gx", "gy"),
            P("member", "gx", "gy"),
        ),
        out_specs=P("member", None, "gx", "gy"),
        check_vma=False,
    )
```
